32 devices in a mesh: dp: 4 (over z), tile: 8 (over y, x, core).
Axes of the slice: x: 2, y: 2, z: 4, core: 2. Of those that a mesh axis runs over, the one named last changes fastest.
Arguments:
- sensitivity: bfloat16 [2048, 2, 128, 128], P('dp', None, 'tile'), may hold values from -6 to 6
- diffusivity: float32 [2, 128, 128], P(None, 'tile'), may hold values from 0.02 to 0.16
Outputs:
- smoothed: bfloat16 [2048, 2, 128, 128], P('dp', None, 'tile')
- gram_matrix: float32 [2048, 2048], P('dp', 'tile')
The draws below stay inside these ranges and needn't reach their ends.
All inputs are finite; a program needn't handle non-finite values.
Results may differ from the reference program's by a relative error of at most 0.014.
Values may be sent and summed in bfloat16 or wider, within the bound.
A program may use at most 128 MiB of HBM per device.

```python
import math
import jax
import jax.numpy as jnp
from jax import lax

ROWS_DEV = 512
LAYERS = 2
NY = 128
STEPS = 4
NX = 128
ROWS = 2048
N_DP = 4


def block_scale(key, dims, shards, least, top_value):
    factor_of, own = 1.0, jax.random.fold_in(key, 6)
    for axis_at, shards_of in shards:
        draws = jnp.exp(jax.random.uniform(jax.random.fold_in(own, axis_at), (shards_of,), jnp.float32, least / len(shards), top_value / len(shards)))
        factor_of = factor_of * jnp.repeat(draws, dims[axis_at] // shards_of).reshape([-1 if axis == axis_at else 1 for axis in range(len(dims))])
    return factor_of


def scatter_about(rng, dims, width, limit, pieces=(), dtype=jnp.bfloat16):
    level = block_scale(rng, dims, pieces, -0.22, 0.18) if pieces else 1.0
    entries = jax.random.normal(rng, dims, jnp.float32) * width * level
    return jnp.minimum(jnp.maximum(entries, -limit), limit).astype(dtype)


def setup_inputs(seed: int = 0) -> dict:
    arg_keys = jax.random.split(jax.random.key(seed), 3)
    return {
        "sensitivity": scatter_about(arg_keys[0], (ROWS, LAYERS, NX, NY), 1.0, 6.0, ((0, 4), (2, 8))),
        "diffusivity": jnp.clip(jnp.exp(math.log(0.16) - 2.0794415 * jax.random.uniform(arg_keys[1], (LAYERS, NX, NY), jnp.float32) ** block_scale(arg_keys[1], (LAYERS, NX, NY), ((1, 8),), -0.2, 0.2)), 0.02, 0.16),
    }


def relax_step(field, coeff):
    centre = field[:, :, 1:-1]
    coeff_mid = coeff[:, 1:-1]
    change = 0.5 * (coeff_mid + coeff[:, 2:]) * (field[:, :, 2:] - centre)
    change = change + 0.5 * (coeff_mid + coeff[:, :-2]) * (field[:, :, :-2] - centre)
    padded = jnp.pad(centre, ((0, 0), (1, 1), (0, 0), (0, 0)))
    coeff_pad = jnp.pad(coeff_mid, ((1, 1), (0, 0), (0, 0)))
    change = change + 0.5 * (coeff_mid + coeff_pad[2:]) * (padded[:, 2:] - centre)
    change = change + 0.5 * (coeff_mid + coeff_pad[:-2]) * (padded[:, :-2] - centre)
    padded = jnp.pad(centre, ((0, 0), (0, 0), (0, 0), (1, 1)))
    coeff_pad = jnp.pad(coeff_mid, ((0, 0), (0, 0), (1, 1)))
    change = change + 0.5 * (coeff_mid + coeff_pad[:, :, 2:]) * (padded[:, :, :, 2:] - centre)
    change = change + 0.5 * (coeff_mid + coeff_pad[:, :, :-2]) * (padded[:, :, :, :-2] - centre)
    return centre + change


def smooth_group(group, diffusivity):
    coeff = jnp.pad(diffusivity, ((0, 0), (1, 1), (0, 0)))
    field = group
    for step_index in range(STEPS):
        widened = jnp.pad(field.astype(jnp.float32), ((0, 0), (0, 0), (1, 1), (0, 0)))
        field = relax_step(widened, coeff).astype(jnp.bfloat16)
    return field


def reference(sensitivity, diffusivity):
    groups = sensitivity.reshape(N_DP, ROWS_DEV, LAYERS, NX, NY)
    smoothed = lax.map(lambda group: smooth_group(group, diffusivity), groups)
    smoothed = smoothed.reshape(ROWS, LAYERS, NX, NY)
    flat_sens = sensitivity.reshape(ROWS, LAYERS * NX * NY)
    flat_smooth = smoothed.reshape(ROWS, LAYERS * NX * NY)
    total = lax.dot_general(flat_sens, flat_smooth, (((1,), (1,)), ((), ())), preferred_element_type=jnp.float32)
    gram_matrix = total / (LAYERS * NX * NY)
    return smoothed, gram_matrix
```

```python
import jax
import jax.numpy as jnp
from jax import lax
from jax.experimental import pallas as pl
from jax.experimental.pallas import tpu as pltpu
from jax.sharding import PartitionSpec as P

STEPS = 4
HALF = 2
MESH = pl.DeviceIdType.MESH
F32 = jnp.float32
BF16 = jnp.bfloat16


def neighbours(block, dim, width, axis="tile"):
    count = lax.axis_size(axis)
    forward = [(i, i + 1) for i in range(count - 1)]
    backward = [(t, s) for s, t in forward]
    low = lax.ppermute(
        lax.slice_in_dim(block, block.shape[dim] - width, None, axis=dim), axis, forward
    )
    high = lax.ppermute(lax.slice_in_dim(block, 0, width, axis=dim), axis, backward)
    return low, high


def extended(block, dim, width):
    low, high = neighbours(block, dim, width)
    return jnp.concatenate([low, block, high], axis=dim)


def coefficients(diffusivity):
    layers, width, ny = diffusivity.shape
    d = extended(diffusivity, 1, HALF)
    tile, tiles = lax.axis_index("tile"), lax.axis_size("tile")
    c = d[:, 1:-1]
    xm = 0.5 * (c + d[:, :-2])
    xp = 0.5 * (c + d[:, 2:])
    cp = jnp.pad(c, ((1, 1), (0, 0), (0, 0)))
    lm = 0.5 * (c + cp[:-2])
    lp = 0.5 * (c + cp[2:])
    cy = jnp.pad(c, ((0, 0), (0, 0), (1, 1)))
    ym = 0.5 * (c + cy[:, :, :-2])
    yp = 0.5 * (c + cy[:, :, 2:])
    a0 = 1.0 - (xm + xp + lm + lp + ym + yp)
    lay = jnp.arange(layers)[:, None, None]
    col = jnp.arange(ny)[None, None, :]
    other = jnp.where(lay == 0, lp, lm)
    ym = jnp.where(col == 0, 0.0, ym)
    yp = jnp.where(col == ny - 1, 0.0, yp)
    x = jnp.arange(width + 2)[None, :, None]
    inside = ((x > 0) | (tile > 0)) & ((x < width + 1) | (tile < tiles - 1))
    stack = jnp.where(inside[None], jnp.stack([a0, xm, xp, other, ym, yp]), 0.0)
    return stack.reshape(6, layers * (width + 2), ny)


def smooth_kernel(width, main_ref, low_ref, high_ref, coeff_ref, out_ref):
    lanes = 128
    ext = width + 2 * HALF

    def load(layer, x):
        if x < HALF:
            at = (layer * HALF + x) * lanes
            return low_ref[:, at : at + lanes].astype(F32)
        if x >= width + HALF:
            at = (layer * HALF + x - width - HALF) * lanes
            return high_ref[:, at : at + lanes].astype(F32)
        at = (layer * width + x - HALF) * lanes
        return main_ref[:, at : at + lanes].astype(F32)

    def step(read, layer, x, cx):
        at = layer * (width + 2) + cx
        w = [coeff_ref[i, at : at + 1, :] for i in range(6)]
        f = read(layer, x)
        total = w[0] * f + w[1] * read(layer, x - 1) + w[2] * read(layer, x + 1)
        total = total + w[3] * read(1 - layer, x)
        total = total + w[4] * pltpu.roll(f, 1, 1)
        return total + w[5] * pltpu.roll(f, lanes - 1, 1)

    first = {}

    def read_first(layer, x):
        if (layer, x) not in first:
            first[layer, x] = step(load, layer, x, x - 1)
        return first[layer, x]

    for x in range(HALF, width + HALF):
        for layer in range(2):
            value = step(read_first, layer, x, x - 1)
            at = (layer * width + x - HALF) * lanes
            out_ref[:, at : at + lanes] = value.astype(BF16)


def two_steps(main, low, high, coeff, width):
    rows, cells = main.shape
    block = 32
    return pl.pallas_call(
        lambda *refs: smooth_kernel(width, *refs),
        out_shape=jax.ShapeDtypeStruct((rows, cells), BF16),
        grid=(rows // block,),
        in_specs=[
            pl.BlockSpec((block, cells), lambda i: (i, 0)),
            pl.BlockSpec((block, low.shape[1]), lambda i: (i, 0)),
            pl.BlockSpec((block, high.shape[1]), lambda i: (i, 0)),
            pl.BlockSpec(coeff.shape, lambda i: (0, 0, 0)),
        ],
        out_specs=pl.BlockSpec((block, cells), lambda i: (i, 0)),
        cost_estimate=pl.CostEstimate(
            flops=rows * cells * 24, bytes_accessed=rows * cells * 8, transcendentals=0
        ),
        name="two_steps",
    )(main, low, high, coeff)


def flat_halo(flat, width):
    rows, cells = flat.shape
    n = width * 128
    w = HALF * 128
    tops = jnp.concatenate([flat[:, n - w : n], flat[:, 2 * n - w :]], axis=1)
    bottoms = jnp.concatenate([flat[:, :w], flat[:, n : n + w]], axis=1)
    count = lax.axis_size("tile")
    forward = [(i, i + 1) for i in range(count - 1)]
    low = lax.ppermute(tops, "tile", forward)
    high = lax.ppermute(bottoms, "tile", [(t, s) for s, t in forward])
    return low, high


def place_kernel(scale, part_ref, out_ref, recv, total, direct_out, turned_out, direct, turned,
                 s1_send, s1_recv, d_send, t_send, d_recv, t_recv):
    p = lax.axis_index("dp")
    t = lax.axis_index("tile")
    tiles = 8
    u, v = t // 2, t % 2
    inner = (p == 1) | (p == 2)
    outer_of = jnp.where(p < 2, 0, 3)
    inner_of = jnp.where(p < 2, 1, 2)
    far_in = 3 - inner_of
    far_out = 3 - outer_of

    barrier = pltpu.get_barrier_semaphore()

    def greet(n, _):
        @pl.when(n != p * tiles + t)
        def _():
            pl.semaphore_signal(barrier, inc=1, device_id=(n // tiles, n % tiles), device_id_type=MESH)
        return 0

    lax.fori_loop(0, 32, greet, 0)
    pl.semaphore_wait(barrier, 31)

    def stage1(s, slot):
        return pltpu.make_async_remote_copy(
            src_ref=part_ref.at[s], dst_ref=recv.at[slot], send_sem=s1_send.at[slot],
            recv_sem=s1_recv.at[slot], device_id=(p, s), device_id_type=MESH)

    for k in range(1, tiles):
        stage1((t + k) % tiles, k - 1).start()
    total[...] = part_ref[t].astype(F32)
    for k in range(1, tiles):
        stage1((t + k) % tiles, k - 1).wait_recv()
        total[...] += recv[k - 1].astype(F32)

    for b in range(6):
        value = total[b] * scale
        direct_out[b] = value.astype(BF16)
        if b < 5:
            turned_out[b] = value.T.astype(BF16)

    rows_of = [outer_of, inner_of, inner_of, outer_of, outer_of, p]
    cols_of = [inner_of, far_in, far_out, far_in, far_out, p]

    def send_direct(b, action):
        dp, dt = rows_of[b], 2 * cols_of[b] + v
        active = inner if b < 5 else (p >= 0)
        mine = (dp == p) & (dt == t)
        where = direct.at[pl.ds(pl.multiple_of(u * 128, 128), 128), :]
        copy = pltpu.make_async_remote_copy(
            src_ref=direct_out.at[b], dst_ref=where, send_sem=d_send.at[b],
            recv_sem=d_recv.at[u], device_id=(dp, dt), device_id_type=MESH)

        @pl.when(active & jnp.logical_not(mine))
        def _():
            copy.start() if action == 0 else copy.wait_send()

        if action == 0:
            @pl.when(active & mine)
            def _():
                where[...] = direct_out[b]

    def send_turned(b, action):
        dp, dt = cols_of[b], 2 * rows_of[b] + u // 2
        mine = (dp == p) & (dt == t)
        col = u % 2
        slot = v * 2 + col
        copy = pltpu.make_async_remote_copy(
            src_ref=turned_out.at[b], dst_ref=turned.at[slot], send_sem=t_send.at[b],
            recv_sem=t_recv.at[slot], device_id=(dp, dt), device_id_type=MESH)

        @pl.when(inner & jnp.logical_not(mine))
        def _():
            copy.start() if action == 0 else copy.wait_send()

        if action == 0:
            @pl.when(inner & mine)
            def _():
                turned[slot] = turned_out[b]

    for b in (4, 2, 3, 1, 0, 5):
        send_direct(b, 0)
        if b < 5:
            send_turned(b, 0)

    g = t // 2
    same_side = (p < 2) == (g < 2)
    cross = jnp.logical_not(same_side)
    has_direct = cross | (p == g) | jnp.logical_not(inner)
    direct_from = jnp.where(p == g, p, inner_of)
    has_turned = cross | ((p != g) & inner)
    turned_from = jnp.where(cross, far_in, inner_of)

    @pl.when(has_direct)
    def _():
        for uu in range(4):
            @pl.when(jnp.logical_not((direct_from == p) & (2 * uu + v == t)))
            def _():
                pltpu.make_async_remote_copy(
                    src_ref=direct_out.at[0], dst_ref=direct.at[pl.ds(uu * 128, 128), :],
                    send_sem=d_send.at[0], recv_sem=d_recv.at[uu], device_id=(p, t),
                    device_id_type=MESH).wait_recv()
        out_ref[...] = direct[...].astype(F32)

    @pl.when(has_turned)
    def _():
        for vv in range(2):
            for cc in range(2):
                @pl.when(jnp.logical_not((turned_from == p) & (2 * (2 * v + cc) + vv == t)))
                def _():
                    pltpu.make_async_remote_copy(
                        src_ref=turned_out.at[0], dst_ref=turned.at[vv * 2 + cc],
                        send_sem=t_send.at[0], recv_sem=t_recv.at[vv * 2 + cc], device_id=(p, t),
                        device_id_type=MESH).wait_recv()

    for vv in range(2):
        for cc in range(2):
            rr, ll = slice(vv * 256, vv * 256 + 256), slice(cc * 128, cc * 128 + 128)

            @pl.when(has_turned & has_direct)
            def _():
                out_ref[rr, ll] += turned[vv * 2 + cc].astype(F32)

            @pl.when(has_turned & jnp.logical_not(has_direct))
            def _():
                out_ref[rr, ll] = turned[vv * 2 + cc].astype(F32)

    for k in range(1, tiles):
        stage1((t + k) % tiles, k - 1).wait_send()
    for b in range(6):
        send_direct(b, 1)
        if b < 5:
            send_turned(b, 1)


def place(part, scale):
    return pl.pallas_call(
        lambda *refs: place_kernel(scale, *refs),
        out_shape=jax.ShapeDtypeStruct((512, 256), F32),
        in_specs=[pl.BlockSpec(memory_space=pltpu.VMEM)],
        out_specs=pl.BlockSpec(memory_space=pltpu.VMEM),
        scratch_shapes=[
            pltpu.VMEM((7, 6, 128, 256), BF16),
            pltpu.VMEM((6, 128, 256), F32),
            pltpu.VMEM((6, 128, 256), BF16),
            pltpu.VMEM((5, 256, 128), BF16),
            pltpu.VMEM((512, 256), BF16),
            pltpu.VMEM((4, 256, 128), BF16),
            pltpu.SemaphoreType.DMA((7,)),
            pltpu.SemaphoreType.DMA((7,)),
            pltpu.SemaphoreType.DMA((6,)),
            pltpu.SemaphoreType.DMA((5,)),
            pltpu.SemaphoreType.DMA((4,)),
            pltpu.SemaphoreType.DMA((4,)),
        ],
        compiler_params=pltpu.CompilerParams(
            collective_id=0, has_side_effects=True, vmem_limit_bytes=32 * 1024 * 1024
        ),
        name="place",
    )(part)


def gram_dot(a, b):
    return lax.dot_general(a, b, (((1,), (1,)), ((), ())), preferred_element_type=F32)


def four_planes(field, total_cells):
    rows, cells = field.shape
    half = cells // 2
    p = lax.axis_index("dp")
    left = p < 2
    first, second = field[:, :half], field[:, half:]
    keep = jnp.where(left, second, first)
    away = jnp.where(left, first, second)
    across = [(1, 2), (2, 1)]
    inward = [(0, 1), (3, 2)]
    far_in = lax.ppermute(away, "dp", across)
    near_away = lax.ppermute(away, "dp", inward)
    near_keep = lax.ppermute(keep, "dp", inward)
    far_out = lax.ppermute(near_away, "dp", across)
    blocks = [
        gram_dot(near_away, away) + gram_dot(near_keep, keep),
        gram_dot(keep, far_in),
        gram_dot(keep, far_out),
        gram_dot(near_keep, far_in),
        gram_dot(near_keep, far_out),
        gram_dot(field, field),
    ]
    cut = [b.astype(BF16).reshape(4, 128, 2, 256).transpose(0, 2, 1, 3).reshape(8, 128, 256) for b in blocks]
    return place(jnp.stack(cut, axis=1), 1.0 / total_cells)


def ring(field, total_cells):
    rows = field.shape[0]
    count = lax.axis_size("dp")
    pos = lax.axis_index("dp")
    pairs = [(s, (s + 1) % count) for s in range(count)]
    block = jnp.zeros((rows, rows * count), F32)

    def add(block, panel, source):
        return lax.dynamic_update_slice(block, gram_dot(field, panel), (jnp.int32(0), source * rows))

    block = add(block, field, pos)

    def turn(i, carry):
        block, panel = carry
        panel = lax.ppermute(panel, "dp", pairs)
        return add(block, panel, (pos - i) % count), panel

    block, _ = lax.fori_loop(1, count, turn, (block, field))
    cols = block.shape[1] // lax.axis_size("tile")
    own = lax.psum_scatter(block.astype(BF16), "tile", scatter_dimension=1, tiled=True)
    return own.astype(F32) / total_cells


def shards(sensitivity, diffusivity):
    rows, layers, width, ny = sensitivity.shape
    total_cells = layers * width * ny * lax.axis_size("tile")
    coeff = coefficients(diffusivity)
    flat = sensitivity.reshape(rows, layers * width * ny)
    middle = two_steps(flat, *flat_halo(flat, width), coeff, width)
    smoothed = two_steps(middle, *flat_halo(middle, width), coeff, width)
    if lax.axis_size("dp") == 4 and lax.axis_size("tile") == 8 and rows == 512:
        gram = four_planes(middle, total_cells)
    else:
        gram = ring(middle, total_cells)
    return smoothed.reshape(sensitivity.shape), gram


def solution(mesh):
    in_specs = (P("dp", None, "tile", None), P(None, "tile", None))
    out_specs = (P("dp", None, "tile", None), P("dp", "tile"))
    return jax.shard_map(shards, mesh=mesh, in_specs=in_specs, out_specs=out_specs, check_vma=False)
```

```python
import jax
import jax.numpy as jnp
from jax import lax
from jax.experimental import pallas as pl
from jax.experimental.pallas import tpu as pltpu
from jax.sharding import PartitionSpec as P

STEPS = 4
HALF = 2
MESH = pl.DeviceIdType.MESH
F32 = jnp.float32
BF16 = jnp.bfloat16


def neighbours(block, dim, width, axis="tile"):
    count = lax.axis_size(axis)
    forward = [(i, i + 1) for i in range(count - 1)]
    backward = [(t, s) for s, t in forward]
    low = lax.ppermute(
        lax.slice_in_dim(block, block.shape[dim] - width, None, axis=dim), axis, forward
    )
    high = lax.ppermute(lax.slice_in_dim(block, 0, width, axis=dim), axis, backward)
    return low, high


def extended(block, dim, width):
    low, high = neighbours(block, dim, width)
    return jnp.concatenate([low, block, high], axis=dim)


def coefficients(diffusivity):
    layers, width, ny = diffusivity.shape
    d = extended(diffusivity, 1, HALF)
    tile, tiles = lax.axis_index("tile"), lax.axis_size("tile")
    c = d[:, 1:-1]
    xm = 0.5 * (c + d[:, :-2])
    xp = 0.5 * (c + d[:, 2:])
    cp = jnp.pad(c, ((1, 1), (0, 0), (0, 0)))
    lm = 0.5 * (c + cp[:-2])
    lp = 0.5 * (c + cp[2:])
    cy = jnp.pad(c, ((0, 0), (0, 0), (1, 1)))
    ym = 0.5 * (c + cy[:, :, :-2])
    yp = 0.5 * (c + cy[:, :, 2:])
    a0 = 1.0 - (xm + xp + lm + lp + ym + yp)
    lay = jnp.arange(layers)[:, None, None]
    col = jnp.arange(ny)[None, None, :]
    other = jnp.where(lay == 0, lp, lm)
    ym = jnp.where(col == 0, 0.0, ym)
    yp = jnp.where(col == ny - 1, 0.0, yp)
    x = jnp.arange(width + 2)[None, :, None]
    inside = ((x > 0) | (tile > 0)) & ((x < width + 1) | (tile < tiles - 1))
    stack = jnp.where(inside[None], jnp.stack([a0, xm, xp, other, ym, yp]), 0.0)
    return stack.reshape(6, layers * (width + 2), ny)


def smooth_kernel(width, split, main_ref, low_ref, high_ref, coeff_ref, out_ref, *halves):
    lanes = 128
    half = width * lanes

    def load(layer, x):
        if x < HALF:
            at = (layer * HALF + x) * lanes
            return low_ref[:, at : at + lanes].astype(F32)
        if x >= width + HALF:
            at = (layer * HALF + x - width - HALF) * lanes
            return high_ref[:, at : at + lanes].astype(F32)
        at = (layer * width + x - HALF) * lanes
        return main_ref[:, at : at + lanes].astype(F32)

    def step(read, layer, x, cx):
        at = layer * (width + 2) + cx
        w = [coeff_ref[i, at : at + 1, :] for i in range(6)]
        f = read(layer, x)
        total = w[0] * f + w[1] * read(layer, x - 1) + w[2] * read(layer, x + 1)
        total = total + w[3] * read(1 - layer, x)
        total = total + w[4] * pltpu.roll(f, 1, 1)
        return total + w[5] * pltpu.roll(f, lanes - 1, 1)

    first = {}

    def read_first(layer, x):
        if (layer, x) not in first:
            first[layer, x] = step(load, layer, x, x - 1)
        return first[layer, x]

    for x in range(HALF, width + HALF):
        for layer in range(2):
            value = step(read_first, layer, x, x - 1)
            at = (layer * width + x - HALF) * lanes
            out_ref[:, at : at + lanes] = value.astype(BF16)
    if split:
        away_ref, keep_ref = halves
        left = 2 * lax.axis_index("dp") < lax.axis_size("dp")

        @pl.when(left)
        def _():
            away_ref[...] = out_ref[:, :half]
            keep_ref[...] = out_ref[:, half:]

        @pl.when(jnp.logical_not(left))
        def _():
            away_ref[...] = out_ref[:, half:]
            keep_ref[...] = out_ref[:, :half]


def two_steps(main, low, high, coeff, width, split):
    rows, cells = main.shape
    block = 32
    outs = [cells] + ([cells // 2] * 2 if split else [])
    return pl.pallas_call(
        lambda *refs: smooth_kernel(width, split, *refs),
        out_shape=[jax.ShapeDtypeStruct((rows, n), BF16) for n in outs],
        grid=(rows // block,),
        in_specs=[
            pl.BlockSpec((block, cells), lambda i: (i, 0)),
            pl.BlockSpec((block, low.shape[1]), lambda i: (i, 0)),
            pl.BlockSpec((block, high.shape[1]), lambda i: (i, 0)),
            pl.BlockSpec(coeff.shape, lambda i: (0, 0, 0)),
        ],
        out_specs=[pl.BlockSpec((block, n), lambda i: (i, 0)) for n in outs],
        cost_estimate=pl.CostEstimate(
            flops=rows * cells * 24, bytes_accessed=rows * cells * 8, transcendentals=0
        ),
        name="two_steps",
    )(main, low, high, coeff)


def exchange(tops, bottoms):
    count = lax.axis_size("tile")
    forward = [(i, i + 1) for i in range(count - 1)]
    low = lax.ppermute(tops, "tile", forward)
    high = lax.ppermute(bottoms, "tile", [(t, s) for s, t in forward])
    return low, high


def flat_halo(flat, width):
    n = width * 128
    w = HALF * 128
    tops = jnp.concatenate([flat[:, n - w : n], flat[:, 2 * n - w :]], axis=1)
    bottoms = jnp.concatenate([flat[:, :w], flat[:, n : n + w]], axis=1)
    return exchange(tops, bottoms)


def first_halo(block):
    rows, width = block.shape[0], block.shape[2]
    return exchange(
        block[:, :, width - HALF :].reshape(rows, -1), block[:, :, :HALF].reshape(rows, -1)
    )


def place_kernel(scale, *refs):
    blocks, out_ref = refs[:6], refs[6]
    (partner, half_out, quarter, direct_out, turned_out, direct, turned,
     s1_send, s1_recv, s2_send, s2_recv, d_send, t_send, d_recv, t_recv) = refs[7:]
    p = lax.axis_index("dp")
    t = lax.axis_index("tile")
    tiles = 8
    u, v = t // 2, t % 2
    inner = (p == 1) | (p == 2)
    outer_of = jnp.where(p < 2, 0, 3)
    inner_of = jnp.where(p < 2, 1, 2)
    far_in = 3 - inner_of
    far_out = 3 - outer_of

    barrier = pltpu.get_barrier_semaphore()

    def greet(n, _):
        @pl.when(n != p * tiles + t)
        def _():
            pl.semaphore_signal(barrier, inc=1, device_id=(n // tiles, n % tiles), device_id_type=MESH)
        return 0

    lax.fori_loop(0, 32, greet, 0)
    pl.semaphore_wait(barrier, 31)

    def when_active(b, run):
        if b == 5:
            run()
        else:
            pl.when(inner)(run)

    own_cols = pl.ds(pl.multiple_of(v * 256, 256), 256)
    other_cols = pl.ds(pl.multiple_of((1 - v) * 256, 256), 256)
    own_rows = pl.ds(pl.multiple_of(u * 128, 128), 128)

    def stage1(b):
        return pltpu.make_async_remote_copy(
            src_ref=blocks[b].at[:, other_cols], dst_ref=partner.at[b], send_sem=s1_send.at[b],
            recv_sem=s1_recv.at[b], device_id=(p, 2 * u + 1 - v), device_id_type=MESH)

    def stage2(b, k):
        to = (u + k) % 4
        return pltpu.make_async_remote_copy(
            src_ref=half_out.at[b, pl.ds(pl.multiple_of(to * 128, 128), 128), :],
            dst_ref=quarter.at[b, k - 1], send_sem=s2_send.at[b, k - 1],
            recv_sem=s2_recv.at[b, k - 1], device_id=(p, 2 * to + v), device_id_type=MESH)

    rows_of = [outer_of, inner_of, inner_of, outer_of, outer_of, p]
    cols_of = [inner_of, far_in, far_out, far_in, far_out, p]

    def send_direct(b, action):
        dp, dt = rows_of[b], 2 * cols_of[b] + v
        active = inner if b < 5 else (p >= 0)
        mine = (dp == p) & (dt == t)
        where = direct.at[pl.ds(pl.multiple_of(u * 128, 128), 128), :]
        copy = pltpu.make_async_remote_copy(
            src_ref=direct_out.at[b], dst_ref=where, send_sem=d_send.at[b],
            recv_sem=d_recv.at[u], device_id=(dp, dt), device_id_type=MESH)

        @pl.when(active & jnp.logical_not(mine))
        def _():
            copy.start() if action == 0 else copy.wait_send()

        if action == 0:
            @pl.when(active & mine)
            def _():
                where[...] = direct_out[b]

    def send_turned(b, action):
        dp, dt = cols_of[b], 2 * rows_of[b] + u // 2
        mine = (dp == p) & (dt == t)
        col = u % 2
        slot = v * 2 + col
        copy = pltpu.make_async_remote_copy(
            src_ref=turned_out.at[b], dst_ref=turned.at[slot], send_sem=t_send.at[b],
            recv_sem=t_recv.at[slot], device_id=(dp, dt), device_id_type=MESH)

        @pl.when(inner & jnp.logical_not(mine))
        def _():
            copy.start() if action == 0 else copy.wait_send()

        if action == 0:
            @pl.when(inner & mine)
            def _():
                turned[slot] = turned_out[b]

    order = (1, 3, 0, 2, 4, 5)
    for b in order:
        when_active(b, lambda b=b: stage1(b).start())
    for b in order:
        def add_partner(b=b):
            stage1(b).wait_recv()
            half_out[b] = (blocks[b][:, own_cols].astype(F32) + partner[b].astype(F32)).astype(BF16)
            for k in range(1, 4):
                stage2(b, k).start()
        when_active(b, add_partner)
    for b in order:
        def finish(b=b):
            value = blocks[b][own_rows, own_cols].astype(F32) + partner[b, own_rows, :].astype(F32)
            for k in range(1, 4):
                stage2(b, k).wait_recv()
                value = value + quarter[b, k - 1].astype(F32)
            value = value * scale
            direct_out[b] = value.astype(BF16)
            if b < 5:
                turned_out[b] = value.T.astype(BF16)
        when_active(b, finish)
        send_direct(b, 0)
        if b < 5:
            send_turned(b, 0)

    g = t // 2
    same_side = (p < 2) == (g < 2)
    cross = jnp.logical_not(same_side)
    has_direct = cross | (p == g) | jnp.logical_not(inner)
    direct_from = jnp.where(p == g, p, inner_of)
    has_turned = cross | ((p != g) & inner)
    turned_from = jnp.where(cross, far_in, inner_of)

    @pl.when(has_direct)
    def _():
        for uu in range(4):
            @pl.when(jnp.logical_not((direct_from == p) & (2 * uu + v == t)))
            def _():
                pltpu.make_async_remote_copy(
                    src_ref=direct_out.at[0], dst_ref=direct.at[pl.ds(uu * 128, 128), :],
                    send_sem=d_send.at[0], recv_sem=d_recv.at[uu], device_id=(p, t),
                    device_id_type=MESH).wait_recv()
        out_ref[...] = direct[...].astype(F32)

    @pl.when(has_turned)
    def _():
        for vv in range(2):
            for cc in range(2):
                @pl.when(jnp.logical_not((turned_from == p) & (2 * (2 * v + cc) + vv == t)))
                def _():
                    pltpu.make_async_remote_copy(
                        src_ref=turned_out.at[0], dst_ref=turned.at[vv * 2 + cc],
                        send_sem=t_send.at[0], recv_sem=t_recv.at[vv * 2 + cc], device_id=(p, t),
                        device_id_type=MESH).wait_recv()

    for vv in range(2):
        for cc in range(2):
            rr, ll = slice(vv * 256, vv * 256 + 256), slice(cc * 128, cc * 128 + 128)

            @pl.when(has_turned & has_direct)
            def _():
                out_ref[rr, ll] += turned[vv * 2 + cc].astype(F32)

            @pl.when(has_turned & jnp.logical_not(has_direct))
            def _():
                out_ref[rr, ll] = turned[vv * 2 + cc].astype(F32)

    for b in range(6):
        def sent(b=b):
            stage1(b).wait_send()
            for k in range(1, 4):
                stage2(b, k).wait_send()
        when_active(b, sent)
        send_direct(b, 1)
        if b < 5:
            send_turned(b, 1)


def place(blocks, scale):
    return pl.pallas_call(
        lambda *refs: place_kernel(scale, *refs),
        out_shape=jax.ShapeDtypeStruct((512, 256), F32),
        in_specs=[pl.BlockSpec(memory_space=pltpu.VMEM)] * 6,
        out_specs=pl.BlockSpec(memory_space=pltpu.VMEM),
        scratch_shapes=[
            pltpu.VMEM((6, 512, 256), BF16),
            pltpu.VMEM((6, 512, 256), BF16),
            pltpu.VMEM((6, 3, 128, 256), BF16),
            pltpu.VMEM((6, 128, 256), BF16),
            pltpu.VMEM((5, 256, 128), BF16),
            pltpu.VMEM((512, 256), BF16),
            pltpu.VMEM((4, 256, 128), BF16),
            pltpu.SemaphoreType.DMA((6,)),
            pltpu.SemaphoreType.DMA((6,)),
            pltpu.SemaphoreType.DMA((6, 3)),
            pltpu.SemaphoreType.DMA((6, 3)),
            pltpu.SemaphoreType.DMA((6,)),
            pltpu.SemaphoreType.DMA((5,)),
            pltpu.SemaphoreType.DMA((4,)),
            pltpu.SemaphoreType.DMA((4,)),
        ],
        compiler_params=pltpu.CompilerParams(
            collective_id=0, has_side_effects=True, vmem_limit_bytes=32 * 1024 * 1024
        ),
        name="place",
    )(*blocks)


def gram_dot(a, b):
    return lax.dot_general(a, b, (((1,), (1,)), ((), ())), preferred_element_type=F32)


def four_planes(away, keep, total_cells):
    across = [(1, 2), (2, 1)]
    inward = [(0, 1), (3, 2)]
    far_in = lax.ppermute(away, "dp", across)
    near_away = lax.ppermute(away, "dp", inward)
    near_keep = lax.ppermute(keep, "dp", inward)
    far_out = lax.ppermute(near_away, "dp", across)
    blocks = [
        gram_dot(near_away, away) + gram_dot(near_keep, keep),
        gram_dot(keep, far_in),
        gram_dot(keep, far_out),
        gram_dot(near_keep, far_in),
        gram_dot(near_keep, far_out),
        gram_dot(away, away) + gram_dot(keep, keep),
    ]
    return place([b.astype(BF16) for b in blocks], 1.0 / total_cells)


def ring(field, total_cells):
    rows = field.shape[0]
    count = lax.axis_size("dp")
    pos = lax.axis_index("dp")
    pairs = [(s, (s + 1) % count) for s in range(count)]
    block = jnp.zeros((rows, rows * count), F32)

    def add(block, panel, source):
        return lax.dynamic_update_slice(block, gram_dot(field, panel), (jnp.int32(0), source * rows))

    block = add(block, field, pos)

    def turn(i, carry):
        block, panel = carry
        panel = lax.ppermute(panel, "dp", pairs)
        return add(block, panel, (pos - i) % count), panel

    block, _ = lax.fori_loop(1, count, turn, (block, field))
    cols = block.shape[1] // lax.axis_size("tile")
    own = lax.psum_scatter(block.astype(BF16), "tile", scatter_dimension=1, tiled=True)
    return own.astype(F32) / total_cells


def shards(sensitivity, diffusivity):
    rows, layers, width, ny = sensitivity.shape
    total_cells = layers * width * ny * lax.axis_size("tile")
    coeff = coefficients(diffusivity)
    flat = sensitivity.reshape(rows, layers * width * ny)
    planes = lax.axis_size("dp") == 4 and lax.axis_size("tile") == 8 and rows == 512
    middle, *halves = two_steps(flat, *first_halo(sensitivity), coeff, width, planes)
    (smoothed,) = two_steps(middle, *flat_halo(middle, width), coeff, width, False)
    if planes:
        gram = four_planes(*halves, total_cells)
    else:
        gram = ring(middle, total_cells)
    return smoothed.reshape(sensitivity.shape), gram


def solution(mesh):
    in_specs = (P("dp", None, "tile", None), P(None, "tile", None))
    out_specs = (P("dp", None, "tile", None), P("dp", "tile"))
    return jax.shard_map(shards, mesh=mesh, in_specs=in_specs, out_specs=out_specs, check_vma=False)
```

```python
import jax
import jax.numpy as jnp
from jax import lax
from jax.experimental import pallas as pl
from jax.experimental.pallas import tpu as pltpu
from jax.sharding import PartitionSpec as P

STEPS = 4
HALF = 2
MESH = pl.DeviceIdType.MESH
F32 = jnp.float32
BF16 = jnp.bfloat16


def neighbours(block, dim, width, axis="tile"):
    count = lax.axis_size(axis)
    forward = [(i, i + 1) for i in range(count - 1)]
    backward = [(t, s) for s, t in forward]
    low = lax.ppermute(
        lax.slice_in_dim(block, block.shape[dim] - width, None, axis=dim), axis, forward
    )
    high = lax.ppermute(lax.slice_in_dim(block, 0, width, axis=dim), axis, backward)
    return low, high


def extended(block, dim, width):
    low, high = neighbours(block, dim, width)
    return jnp.concatenate([low, block, high], axis=dim)


def coefficients(diffusivity):
    layers, width, ny = diffusivity.shape
    d = extended(diffusivity, 1, HALF)
    tile, tiles = lax.axis_index("tile"), lax.axis_size("tile")
    c = d[:, 1:-1]
    xm = 0.5 * (c + d[:, :-2])
    xp = 0.5 * (c + d[:, 2:])
    cp = jnp.pad(c, ((1, 1), (0, 0), (0, 0)))
    lm = 0.5 * (c + cp[:-2])
    lp = 0.5 * (c + cp[2:])
    cy = jnp.pad(c, ((0, 0), (0, 0), (1, 1)))
    ym = 0.5 * (c + cy[:, :, :-2])
    yp = 0.5 * (c + cy[:, :, 2:])
    a0 = 1.0 - (xm + xp + lm + lp + ym + yp)
    lay = jnp.arange(layers)[:, None, None]
    col = jnp.arange(ny)[None, None, :]
    other = jnp.where(lay == 0, lp, lm)
    ym = jnp.where(col == 0, 0.0, ym)
    yp = jnp.where(col == ny - 1, 0.0, yp)
    x = jnp.arange(width + 2)[None, :, None]
    inside = ((x > 0) | (tile > 0)) & ((x < width + 1) | (tile < tiles - 1))
    stack = jnp.where(inside[None], jnp.stack([a0, xm, xp, other, ym, yp]), 0.0)
    return stack.reshape(6, layers * (width + 2), ny)


def smooth_kernel(width, split, main_ref, low_ref, high_ref, coeff_ref, out_ref, *halves):
    lanes = 128
    half = width * lanes

    def load(layer, x):
        if x < HALF:
            at = (layer * HALF + x) * lanes
            return low_ref[:, at : at + lanes].astype(F32)
        if x >= width + HALF:
            at = (layer * HALF + x - width - HALF) * lanes
            return high_ref[:, at : at + lanes].astype(F32)
        at = (layer * width + x - HALF) * lanes
        return main_ref[:, at : at + lanes].astype(F32)

    def step(read, layer, x, cx):
        at = layer * (width + 2) + cx
        w = [coeff_ref[i, at : at + 1, :] for i in range(6)]
        f = read(layer, x)
        total = w[0] * f + w[1] * read(layer, x - 1) + w[2] * read(layer, x + 1)
        total = total + w[3] * read(1 - layer, x)
        total = total + w[4] * pltpu.roll(f, 1, 1)
        return total + w[5] * pltpu.roll(f, lanes - 1, 1)

    first = {}

    def read_first(layer, x):
        if (layer, x) not in first:
            first[layer, x] = step(load, layer, x, x - 1)
        return first[layer, x]

    for x in range(HALF, width + HALF):
        for layer in range(2):
            value = step(read_first, layer, x, x - 1)
            at = (layer * width + x - HALF) * lanes
            out_ref[:, at : at + lanes] = value.astype(BF16)
    if split:
        away_ref, keep_ref = halves
        left = 2 * lax.axis_index("dp") < lax.axis_size("dp")

        @pl.when(left)
        def _():
            away_ref[...] = out_ref[:, :half]
            keep_ref[...] = out_ref[:, half:]

        @pl.when(jnp.logical_not(left))
        def _():
            away_ref[...] = out_ref[:, half:]
            keep_ref[...] = out_ref[:, :half]


def two_steps(main, low, high, coeff, width, split):
    rows, cells = main.shape
    block = 32
    outs = [cells] + ([cells // 2] * 2 if split else [])
    return pl.pallas_call(
        lambda *refs: smooth_kernel(width, split, *refs),
        out_shape=[jax.ShapeDtypeStruct((rows, n), BF16) for n in outs],
        grid=(rows // block,),
        in_specs=[
            pl.BlockSpec((block, cells), lambda i: (i, 0)),
            pl.BlockSpec((block, low.shape[1]), lambda i: (i, 0)),
            pl.BlockSpec((block, high.shape[1]), lambda i: (i, 0)),
            pl.BlockSpec(coeff.shape, lambda i: (0, 0, 0)),
        ],
        out_specs=[pl.BlockSpec((block, n), lambda i: (i, 0)) for n in outs],
        cost_estimate=pl.CostEstimate(
            flops=rows * cells * 24, bytes_accessed=rows * cells * 8, transcendentals=0
        ),
        name="two_steps",
    )(main, low, high, coeff)


def exchange(tops, bottoms):
    count = lax.axis_size("tile")
    forward = [(i, i + 1) for i in range(count - 1)]
    low = lax.ppermute(tops, "tile", forward)
    high = lax.ppermute(bottoms, "tile", [(t, s) for s, t in forward])
    return low, high


def flat_halo(flat, width):
    n = width * 128
    w = HALF * 128
    tops = jnp.concatenate([flat[:, n - w : n], flat[:, 2 * n - w :]], axis=1)
    bottoms = jnp.concatenate([flat[:, :w], flat[:, n : n + w]], axis=1)
    return exchange(tops, bottoms)


def first_halo(block):
    rows, width = block.shape[0], block.shape[2]
    return exchange(
        block[:, :, width - HALF :].reshape(rows, -1), block[:, :, :HALF].reshape(rows, -1)
    )


def place_kernel(scale, late, *refs):
    order = (3, 0, 2, 4) if late else (1, 5)
    slot_of = {b: n for n, b in enumerate(order)}
    if late:
        near_ref, far_in_ref, far_out_ref, keep_ref, begun_ref, early_ref = refs[:6]
        refs = refs[6:]
    else:
        block_refs, refs = refs[:2], refs[2:]
    (out_ref, outgoing, own, partner, half_out, quarter, direct_out, turned_out, direct, turned,
     s1_send, s1_recv, s2_send, s2_recv, d_send, t_send, d_recv, t_recv) = refs

    def product(b, cols):
        if not late:
            return block_refs[slot_of[b]][:, cols].astype(F32)
        rows_ref = keep_ref if b == 2 else near_ref
        cols_ref = {0: keep_ref, 2: far_out_ref, 3: far_in_ref, 4: far_out_ref}[b]
        value = gram_dot(rows_ref[...], cols_ref[cols, :])
        return value + begun_ref[:, cols] if b == 0 else value
    p = lax.axis_index("dp")
    t = lax.axis_index("tile")
    tiles = 8
    u, v = t // 2, t % 2
    inner = (p == 1) | (p == 2)
    outer_of = jnp.where(p < 2, 0, 3)
    inner_of = jnp.where(p < 2, 1, 2)
    far_in = 3 - inner_of
    far_out = 3 - outer_of

    barrier = pltpu.get_barrier_semaphore()

    def greet(n, _):
        @pl.when(n != p * tiles + t)
        def _():
            pl.semaphore_signal(barrier, inc=1, device_id=(n // tiles, n % tiles), device_id_type=MESH)
        return 0

    lax.fori_loop(0, 32, greet, 0)
    pl.semaphore_wait(barrier, 31)

    def when_active(b, run):
        if b == 5:
            run()
        else:
            pl.when(inner)(run)

    own_cols = pl.ds(pl.multiple_of(v * 256, 256), 256)
    other_cols = pl.ds(pl.multiple_of((1 - v) * 256, 256), 256)
    own_rows = pl.ds(pl.multiple_of(u * 128, 128), 128)

    def stage1(b):
        n = slot_of[b]
        return pltpu.make_async_remote_copy(
            src_ref=outgoing.at[n], dst_ref=partner.at[n], send_sem=s1_send.at[n],
            recv_sem=s1_recv.at[n], device_id=(p, 2 * u + 1 - v), device_id_type=MESH)

    def stage2(b, k):
        n = slot_of[b]
        to = (u + k) % 4
        return pltpu.make_async_remote_copy(
            src_ref=half_out.at[n, pl.ds(pl.multiple_of(to * 128, 128), 128), :],
            dst_ref=quarter.at[n, k - 1], send_sem=s2_send.at[n, k - 1],
            recv_sem=s2_recv.at[n, k - 1], device_id=(p, 2 * to + v), device_id_type=MESH)

    rows_of = [outer_of, inner_of, inner_of, outer_of, outer_of, p]
    cols_of = [inner_of, far_in, far_out, far_in, far_out, p]

    def send_direct(b, action):
        dp, dt = rows_of[b], 2 * cols_of[b] + v
        active = inner if b < 5 else (p >= 0)
        mine = (dp == p) & (dt == t)
        where = direct.at[pl.ds(pl.multiple_of(u * 128, 128), 128), :]
        copy = pltpu.make_async_remote_copy(
            src_ref=direct_out.at[slot_of[b]], dst_ref=where, send_sem=d_send.at[slot_of[b]],
            recv_sem=d_recv.at[u], device_id=(dp, dt), device_id_type=MESH)

        @pl.when(active & jnp.logical_not(mine))
        def _():
            copy.start() if action == 0 else copy.wait_send()

        if action == 0:
            @pl.when(active & mine)
            def _():
                where[...] = direct_out[slot_of[b]]

    def send_turned(b, action):
        dp, dt = cols_of[b], 2 * rows_of[b] + u // 2
        mine = (dp == p) & (dt == t)
        col = u % 2
        slot = v * 2 + col
        copy = pltpu.make_async_remote_copy(
            src_ref=turned_out.at[slot_of[b]], dst_ref=turned.at[slot], send_sem=t_send.at[slot_of[b]],
            recv_sem=t_recv.at[slot], device_id=(dp, dt), device_id_type=MESH)

        @pl.when(inner & jnp.logical_not(mine))
        def _():
            copy.start() if action == 0 else copy.wait_send()

        if action == 0:
            @pl.when(inner & mine)
            def _():
                turned[slot] = turned_out[slot_of[b]]

    for b in order:
        def begin(b=b):
            outgoing[slot_of[b]] = product(b, other_cols).astype(BF16)
            stage1(b).start()
        when_active(b, begin)
    for b in order:
        def add_partner(b=b):
            n = slot_of[b]
            own[n] = product(b, own_cols)
            stage1(b).wait_recv()
            half_out[n] = (own[n] + partner[n].astype(F32)).astype(BF16)
            for k in range(1, 4):
                stage2(b, k).start()
        when_active(b, add_partner)
    for b in order:
        def finish(b=b):
            n = slot_of[b]
            value = own[n, own_rows, :] + partner[n, own_rows, :].astype(F32)
            for k in range(1, 4):
                stage2(b, k).wait_recv()
                value = value + quarter[n, k - 1].astype(F32)
            value = value * scale
            direct_out[n] = value.astype(BF16)
            if b < 5:
                turned_out[n] = value.T.astype(BF16)
        when_active(b, finish)
        send_direct(b, 0)
        if b < 5:
            send_turned(b, 0)

    g = t // 2
    same_side = (p < 2) == (g < 2)
    cross = jnp.logical_not(same_side)
    has_direct = cross | (p == g) | jnp.logical_not(inner)
    direct_from = jnp.where(p == g, p, inner_of)
    has_turned = cross | ((p != g) & inner)
    turned_from = jnp.where(cross, far_in, inner_of)
    middle_pair = cross & inner & ((g == 1) | (g == 2))
    early_cell = middle_pair | (p == g)
    mine_now = jnp.logical_not(early_cell) if late else early_cell
    has_direct = has_direct & mine_now
    has_turned = has_turned & mine_now
    if late:
        @pl.when(early_cell)
        def _():
            out_ref[...] = early_ref[...]
    else:
        @pl.when(jnp.logical_not(early_cell))
        def _():
            out_ref[...] = jnp.zeros_like(out_ref)

    @pl.when(has_direct)
    def _():
        for uu in range(4):
            @pl.when(jnp.logical_not((direct_from == p) & (2 * uu + v == t)))
            def _():
                pltpu.make_async_remote_copy(
                    src_ref=direct_out.at[0], dst_ref=direct.at[pl.ds(uu * 128, 128), :],
                    send_sem=d_send.at[0], recv_sem=d_recv.at[uu], device_id=(p, t),
                    device_id_type=MESH).wait_recv()
        out_ref[...] = direct[...].astype(F32)

    @pl.when(has_turned)
    def _():
        for vv in range(2):
            for cc in range(2):
                @pl.when(jnp.logical_not((turned_from == p) & (2 * (2 * v + cc) + vv == t)))
                def _():
                    pltpu.make_async_remote_copy(
                        src_ref=turned_out.at[0], dst_ref=turned.at[vv * 2 + cc],
                        send_sem=t_send.at[0], recv_sem=t_recv.at[vv * 2 + cc], device_id=(p, t),
                        device_id_type=MESH).wait_recv()

    for vv in range(2):
        for cc in range(2):
            rr, ll = slice(vv * 256, vv * 256 + 256), slice(cc * 128, cc * 128 + 128)

            @pl.when(has_turned & has_direct)
            def _():
                out_ref[rr, ll] += turned[vv * 2 + cc].astype(F32)

            @pl.when(has_turned & jnp.logical_not(has_direct))
            def _():
                out_ref[rr, ll] = turned[vv * 2 + cc].astype(F32)

    for b in order:
        def sent(b=b):
            stage1(b).wait_send()
            for k in range(1, 4):
                stage2(b, k).wait_send()
        when_active(b, sent)
        send_direct(b, 1)
        if b < 5:
            send_turned(b, 1)


def place(operands, scale, late):
    n = 4 if late else 2
    return pl.pallas_call(
        lambda *refs: place_kernel(scale, late, *refs),
        out_shape=jax.ShapeDtypeStruct((512, 256), F32),
        in_specs=[pl.BlockSpec(memory_space=pltpu.VMEM)] * len(operands),
        out_specs=pl.BlockSpec(memory_space=pltpu.VMEM),
        scratch_shapes=[
            pltpu.VMEM((n, 512, 256), BF16),
            pltpu.VMEM((n, 512, 256), F32),
            pltpu.VMEM((n, 512, 256), BF16),
            pltpu.VMEM((n, 512, 256), BF16),
            pltpu.VMEM((n, 3, 128, 256), BF16),
            pltpu.VMEM((n, 128, 256), BF16),
            pltpu.VMEM((n, 256, 128), BF16),
            pltpu.VMEM((512, 256), BF16),
            pltpu.VMEM((4, 256, 128), BF16),
            pltpu.SemaphoreType.DMA((n,)),
            pltpu.SemaphoreType.DMA((n,)),
            pltpu.SemaphoreType.DMA((n, 3)),
            pltpu.SemaphoreType.DMA((n, 3)),
            pltpu.SemaphoreType.DMA((n,)),
            pltpu.SemaphoreType.DMA((n,)),
            pltpu.SemaphoreType.DMA((4,)),
            pltpu.SemaphoreType.DMA((4,)),
        ],
        compiler_params=pltpu.CompilerParams(
            collective_id=int(late), has_side_effects=True, vmem_limit_bytes=40 * 1024 * 1024
        ),
        cost_estimate=pl.CostEstimate(flops=0, bytes_accessed=50_000_000, transcendentals=0),
        name="place_late" if late else "place_early",
    )(*operands)


def gram_dot(a, b):
    return lax.dot_general(a, b, (((1,), (1,)), ((), ())), preferred_element_type=F32)


def four_planes(field, away, keep, smoothed, total_cells):
    across = [(1, 2), (2, 1)]
    inward = [(0, 1), (3, 2)]
    far_in = lax.ppermute(away, "dp", across)
    near_away = lax.ppermute(away, "dp", inward)
    near_keep = lax.ppermute(keep, "dp", inward)
    far_out = lax.ppermute(near_away, "dp", across)
    scale = 1.0 / total_cells
    begun = gram_dot(near_away, away)
    early = [gram_dot(keep, far_in).astype(BF16), gram_dot(field, field).astype(BF16)]
    early = place(early, scale, False)
    near_keep, far_out, far_in, begun, early, smoothed = lax.optimization_barrier(
        (near_keep, far_out, far_in, begun, early, smoothed)
    )
    gram = place((near_keep, far_in, far_out, keep, begun, early), scale, True)
    return smoothed, gram


def ring(field, total_cells):
    rows = field.shape[0]
    count = lax.axis_size("dp")
    pos = lax.axis_index("dp")
    pairs = [(s, (s + 1) % count) for s in range(count)]
    block = jnp.zeros((rows, rows * count), F32)

    def add(block, panel, source):
        return lax.dynamic_update_slice(block, gram_dot(field, panel), (jnp.int32(0), source * rows))

    block = add(block, field, pos)

    def turn(i, carry):
        block, panel = carry
        panel = lax.ppermute(panel, "dp", pairs)
        return add(block, panel, (pos - i) % count), panel

    block, _ = lax.fori_loop(1, count, turn, (block, field))
    cols = block.shape[1] // lax.axis_size("tile")
    own = lax.psum_scatter(block.astype(BF16), "tile", scatter_dimension=1, tiled=True)
    return own.astype(F32) / total_cells


def shards(sensitivity, diffusivity):
    rows, layers, width, ny = sensitivity.shape
    total_cells = layers * width * ny * lax.axis_size("tile")
    coeff = coefficients(diffusivity)
    flat = sensitivity.reshape(rows, layers * width * ny)
    planes = lax.axis_size("dp") == 4 and lax.axis_size("tile") == 8 and rows == 512
    middle, *halves = two_steps(flat, *first_halo(sensitivity), coeff, width, planes)
    (smoothed,) = two_steps(middle, *flat_halo(middle, width), coeff, width, False)
    if planes:
        smoothed, gram = four_planes(
            middle, *halves, smoothed.reshape(sensitivity.shape), total_cells
        )
    else:
        gram = ring(middle, total_cells)
    return smoothed.reshape(sensitivity.shape), gram


def solution(mesh):
    in_specs = (P("dp", None, "tile", None), P(None, "tile", None))
    out_specs = (P("dp", None, "tile", None), P("dp", "tile"))
    return jax.shard_map(shards, mesh=mesh, in_specs=in_specs, out_specs=out_specs, check_vma=False)
```

```python
import jax
import jax.numpy as jnp
from jax import lax
from jax.experimental import pallas as pl
from jax.experimental.pallas import tpu as pltpu
from jax.sharding import PartitionSpec as P

STEPS = 4
HALF = 2
MESH = pl.DeviceIdType.MESH
F32 = jnp.float32
BF16 = jnp.bfloat16


def neighbours(block, dim, width, axis="tile"):
    count = lax.axis_size(axis)
    forward = [(i, i + 1) for i in range(count - 1)]
    backward = [(t, s) for s, t in forward]
    low = lax.ppermute(
        lax.slice_in_dim(block, block.shape[dim] - width, None, axis=dim), axis, forward
    )
    high = lax.ppermute(lax.slice_in_dim(block, 0, width, axis=dim), axis, backward)
    return low, high


def extended(block, dim, width):
    low, high = neighbours(block, dim, width)
    return jnp.concatenate([low, block, high], axis=dim)


def coefficients(diffusivity):
    layers, width, ny = diffusivity.shape
    d = extended(diffusivity, 1, HALF)
    tile, tiles = lax.axis_index("tile"), lax.axis_size("tile")
    c = d[:, 1:-1]
    xm = 0.5 * (c + d[:, :-2])
    xp = 0.5 * (c + d[:, 2:])
    cp = jnp.pad(c, ((1, 1), (0, 0), (0, 0)))
    lm = 0.5 * (c + cp[:-2])
    lp = 0.5 * (c + cp[2:])
    cy = jnp.pad(c, ((0, 0), (0, 0), (1, 1)))
    ym = 0.5 * (c + cy[:, :, :-2])
    yp = 0.5 * (c + cy[:, :, 2:])
    a0 = 1.0 - (xm + xp + lm + lp + ym + yp)
    lay = jnp.arange(layers)[:, None, None]
    col = jnp.arange(ny)[None, None, :]
    other = jnp.where(lay == 0, lp, lm)
    ym = jnp.where(col == 0, 0.0, ym)
    yp = jnp.where(col == ny - 1, 0.0, yp)
    x = jnp.arange(width + 2)[None, :, None]
    inside = ((x > 0) | (tile > 0)) & ((x < width + 1) | (tile < tiles - 1))
    stack = jnp.where(inside[None], jnp.stack([a0, xm, xp, other, ym, yp]), 0.0)
    return stack.reshape(6, layers * (width + 2), ny)


def smooth_kernel(width, split, main_ref, low_ref, high_ref, coeff_ref, out_ref, *halves):
    lanes = 128
    half = width * lanes

    def load(layer, x):
        if x < HALF:
            at = (layer * HALF + x) * lanes
            return low_ref[:, at : at + lanes].astype(F32)
        if x >= width + HALF:
            at = (layer * HALF + x - width - HALF) * lanes
            return high_ref[:, at : at + lanes].astype(F32)
        at = (layer * width + x - HALF) * lanes
        return main_ref[:, at : at + lanes].astype(F32)

    def step(read, layer, x, cx):
        at = layer * (width + 2) + cx
        w = [coeff_ref[i, at : at + 1, :] for i in range(6)]
        f = read(layer, x)
        total = w[0] * f + w[1] * read(layer, x - 1) + w[2] * read(layer, x + 1)
        total = total + w[3] * read(1 - layer, x)
        total = total + w[4] * pltpu.roll(f, 1, 1)
        return total + w[5] * pltpu.roll(f, lanes - 1, 1)

    first = {}

    def read_first(layer, x):
        if (layer, x) not in first:
            first[layer, x] = step(load, layer, x, x - 1)
        return first[layer, x]

    for x in range(HALF, width + HALF):
        for layer in range(2):
            value = step(read_first, layer, x, x - 1)
            at = (layer * width + x - HALF) * lanes
            out_ref[:, at : at + lanes] = value.astype(BF16)
    if split:
        away_ref, keep_ref = halves
        left = 2 * lax.axis_index("dp") < lax.axis_size("dp")

        @pl.when(left)
        def _():
            away_ref[...] = out_ref[:, :half]
            keep_ref[...] = out_ref[:, half:]

        @pl.when(jnp.logical_not(left))
        def _():
            away_ref[...] = out_ref[:, half:]
            keep_ref[...] = out_ref[:, :half]


def two_steps(main, low, high, coeff, width, split):
    rows, cells = main.shape
    block = 32
    outs = [cells] + ([cells // 2] * 2 if split else [])
    return pl.pallas_call(
        lambda *refs: smooth_kernel(width, split, *refs),
        out_shape=[jax.ShapeDtypeStruct((rows, n), BF16) for n in outs],
        grid=(rows // block,),
        in_specs=[
            pl.BlockSpec((block, cells), lambda i: (i, 0)),
            pl.BlockSpec((block, low.shape[1]), lambda i: (i, 0)),
            pl.BlockSpec((block, high.shape[1]), lambda i: (i, 0)),
            pl.BlockSpec(coeff.shape, lambda i: (0, 0, 0)),
        ],
        out_specs=[pl.BlockSpec((block, n), lambda i: (i, 0)) for n in outs],
        cost_estimate=pl.CostEstimate(
            flops=rows * cells * 24, bytes_accessed=rows * cells * 8, transcendentals=0
        ),
        name="two_steps",
    )(main, low, high, coeff)


def exchange(tops, bottoms):
    count = lax.axis_size("tile")
    forward = [(i, i + 1) for i in range(count - 1)]
    low = lax.ppermute(tops, "tile", forward)
    high = lax.ppermute(bottoms, "tile", [(t, s) for s, t in forward])
    return low, high


def flat_halo(flat, width):
    n = width * 128
    w = HALF * 128
    tops = jnp.concatenate([flat[:, n - w : n], flat[:, 2 * n - w :]], axis=1)
    bottoms = jnp.concatenate([flat[:, :w], flat[:, n : n + w]], axis=1)
    return exchange(tops, bottoms)


def first_halo(block):
    rows, width = block.shape[0], block.shape[2]
    return exchange(
        block[:, :, width - HALF :].reshape(rows, -1), block[:, :, :HALF].reshape(rows, -1)
    )


def place_kernel(scale, late, *refs):
    order = (3, 0, 2, 4) if late else (1, 5)
    slot_of = {b: n for n, b in enumerate(order)}
    if late:
        near_ref, far_in_ref, far_out_ref, keep_ref, begun_ref, early_ref = refs[:6]
        refs = refs[6:]
    else:
        block_refs, refs = refs[:2], refs[2:]
    (out_ref, outgoing, own, partner, half_out, quarter, direct_out, turned_out, direct, turned,
     s1_send, s1_recv, s2_send, s2_recv, d_send, t_send, d_recv, t_recv) = refs

    def product(b, cols):
        if not late:
            return block_refs[slot_of[b]][:, cols].astype(F32)
        rows_ref = keep_ref if b == 2 else near_ref
        cols_ref = {0: keep_ref, 2: far_out_ref, 3: far_in_ref, 4: far_out_ref}[b]
        value = gram_dot(rows_ref[...], cols_ref[cols, :])
        return value + begun_ref[:, cols] if b == 0 else value
    p = lax.axis_index("dp")
    t = lax.axis_index("tile")
    tiles = 8
    u, v = t // 2, t % 2
    inner = (p == 1) | (p == 2)
    outer_of = jnp.where(p < 2, 0, 3)
    inner_of = jnp.where(p < 2, 1, 2)
    far_in = 3 - inner_of
    far_out = 3 - outer_of

    barrier = pltpu.get_barrier_semaphore()

    def greet(n, _):
        @pl.when(n != p * tiles + t)
        def _():
            pl.semaphore_signal(barrier, inc=1, device_id=(n // tiles, n % tiles), device_id_type=MESH)
        return 0

    lax.fori_loop(0, 32, greet, 0)
    pl.semaphore_wait(barrier, 31)

    def when_active(b, run):
        if b == 5:
            run()
        else:
            pl.when(inner)(run)

    own_cols = pl.ds(pl.multiple_of(v * 256, 256), 256)
    other_cols = pl.ds(pl.multiple_of((1 - v) * 256, 256), 256)
    own_rows = pl.ds(pl.multiple_of(u * 128, 128), 128)

    def stage1(b):
        n = slot_of[b]
        return pltpu.make_async_remote_copy(
            src_ref=outgoing.at[n], dst_ref=partner.at[n], send_sem=s1_send.at[n],
            recv_sem=s1_recv.at[n], device_id=(p, 2 * u + 1 - v), device_id_type=MESH)

    def stage2(b, k):
        n = slot_of[b]
        to = (u + k) % 4
        return pltpu.make_async_remote_copy(
            src_ref=half_out.at[n, pl.ds(pl.multiple_of(to * 128, 128), 128), :],
            dst_ref=quarter.at[n, k - 1], send_sem=s2_send.at[n, k - 1],
            recv_sem=s2_recv.at[n, k - 1], device_id=(p, 2 * to + v), device_id_type=MESH)

    rows_of = [outer_of, inner_of, inner_of, outer_of, outer_of, p]
    cols_of = [inner_of, far_in, far_out, far_in, far_out, p]

    def send_direct(b, action):
        dp, dt = rows_of[b], 2 * cols_of[b] + v
        active = inner if b < 5 else (p >= 0)
        mine = (dp == p) & (dt == t)
        where = direct.at[pl.ds(pl.multiple_of(u * 128, 128), 128), :]
        copy = pltpu.make_async_remote_copy(
            src_ref=direct_out.at[slot_of[b]], dst_ref=where, send_sem=d_send.at[slot_of[b]],
            recv_sem=d_recv.at[u], device_id=(dp, dt), device_id_type=MESH)

        @pl.when(active & jnp.logical_not(mine))
        def _():
            copy.start() if action == 0 else copy.wait_send()

        if action == 0:
            @pl.when(active & mine)
            def _():
                where[...] = direct_out[slot_of[b]]

    def send_turned(b, action):
        dp, dt = cols_of[b], 2 * rows_of[b] + u // 2
        mine = (dp == p) & (dt == t)
        col = u % 2
        slot = v * 2 + col
        copy = pltpu.make_async_remote_copy(
            src_ref=turned_out.at[slot_of[b]], dst_ref=turned.at[slot], send_sem=t_send.at[slot_of[b]],
            recv_sem=t_recv.at[slot], device_id=(dp, dt), device_id_type=MESH)

        @pl.when(inner & jnp.logical_not(mine))
        def _():
            copy.start() if action == 0 else copy.wait_send()

        if action == 0:
            @pl.when(inner & mine)
            def _():
                turned[slot] = turned_out[slot_of[b]]

    for b in order:
        def begin(b=b):
            outgoing[slot_of[b]] = product(b, other_cols).astype(BF16)
            stage1(b).start()
        when_active(b, begin)
    for b in order:
        def add_partner(b=b):
            n = slot_of[b]
            own[n] = product(b, own_cols)
            stage1(b).wait_recv()
            half_out[n] = (own[n] + partner[n].astype(F32)).astype(BF16)
            for k in range(1, 4):
                stage2(b, k).start()
        when_active(b, add_partner)
    for b in order:
        def finish(b=b):
            n = slot_of[b]
            value = own[n, own_rows, :] + partner[n, own_rows, :].astype(F32)
            for k in range(1, 4):
                stage2(b, k).wait_recv()
                value = value + quarter[n, k - 1].astype(F32)
            value = value * scale
            direct_out[n] = value.astype(BF16)
            if b < 5:
                turned_out[n] = value.T.astype(BF16)
        when_active(b, finish)
        send_direct(b, 0)
        if b < 5:
            send_turned(b, 0)

    g = t // 2
    same_side = (p < 2) == (g < 2)
    cross = jnp.logical_not(same_side)
    has_direct = cross | (p == g) | jnp.logical_not(inner)
    direct_from = jnp.where(p == g, p, inner_of)
    has_turned = cross | ((p != g) & inner)
    turned_from = jnp.where(cross, far_in, inner_of)
    middle_pair = cross & inner & ((g == 1) | (g == 2))
    early_cell = middle_pair | (p == g)
    mine_now = jnp.logical_not(early_cell) if late else early_cell
    has_direct = has_direct & mine_now
    has_turned = has_turned & mine_now
    if late:
        @pl.when(early_cell)
        def _():
            out_ref[...] = early_ref[...]
    else:
        @pl.when(jnp.logical_not(early_cell))
        def _():
            out_ref[...] = jnp.zeros_like(out_ref)

    @pl.when(has_direct)
    def _():
        for uu in range(4):
            @pl.when(jnp.logical_not((direct_from == p) & (2 * uu + v == t)))
            def _():
                pltpu.make_async_remote_copy(
                    src_ref=direct_out.at[0], dst_ref=direct.at[pl.ds(uu * 128, 128), :],
                    send_sem=d_send.at[0], recv_sem=d_recv.at[uu], device_id=(p, t),
                    device_id_type=MESH).wait_recv()
        out_ref[...] = direct[...].astype(F32)

    @pl.when(has_turned)
    def _():
        for vv in range(2):
            for cc in range(2):
                @pl.when(jnp.logical_not((turned_from == p) & (2 * (2 * v + cc) + vv == t)))
                def _():
                    pltpu.make_async_remote_copy(
                        src_ref=turned_out.at[0], dst_ref=turned.at[vv * 2 + cc],
                        send_sem=t_send.at[0], recv_sem=t_recv.at[vv * 2 + cc], device_id=(p, t),
                        device_id_type=MESH).wait_recv()

    for vv in range(2):
        for cc in range(2):
            rr, ll = slice(vv * 256, vv * 256 + 256), slice(cc * 128, cc * 128 + 128)

            @pl.when(has_turned & has_direct)
            def _():
                out_ref[rr, ll] += turned[vv * 2 + cc].astype(F32)

            @pl.when(has_turned & jnp.logical_not(has_direct))
            def _():
                out_ref[rr, ll] = turned[vv * 2 + cc].astype(F32)

    for b in order:
        def sent(b=b):
            stage1(b).wait_send()
            for k in range(1, 4):
                stage2(b, k).wait_send()
        when_active(b, sent)
        send_direct(b, 1)
        if b < 5:
            send_turned(b, 1)


def place(operands, scale, late):
    n = 4 if late else 2
    return pl.pallas_call(
        lambda *refs: place_kernel(scale, late, *refs),
        out_shape=jax.ShapeDtypeStruct((512, 256), F32),
        in_specs=[pl.BlockSpec(memory_space=pltpu.VMEM)] * len(operands),
        out_specs=pl.BlockSpec(memory_space=pltpu.VMEM),
        scratch_shapes=[
            pltpu.VMEM((n, 512, 256), BF16),
            pltpu.VMEM((n, 512, 256), F32),
            pltpu.VMEM((n, 512, 256), BF16),
            pltpu.VMEM((n, 512, 256), BF16),
            pltpu.VMEM((n, 3, 128, 256), BF16),
            pltpu.VMEM((n, 128, 256), BF16),
            pltpu.VMEM((n, 256, 128), BF16),
            pltpu.VMEM((512, 256), BF16),
            pltpu.VMEM((4, 256, 128), BF16),
            pltpu.SemaphoreType.DMA((n,)),
            pltpu.SemaphoreType.DMA((n,)),
            pltpu.SemaphoreType.DMA((n, 3)),
            pltpu.SemaphoreType.DMA((n, 3)),
            pltpu.SemaphoreType.DMA((n,)),
            pltpu.SemaphoreType.DMA((n,)),
            pltpu.SemaphoreType.DMA((4,)),
            pltpu.SemaphoreType.DMA((4,)),
        ],
        compiler_params=pltpu.CompilerParams(
            collective_id=int(late), has_side_effects=True, vmem_limit_bytes=40 * 1024 * 1024
        ),
        cost_estimate=pl.CostEstimate(flops=0, bytes_accessed=50_000_000, transcendentals=0),
        name="place_late" if late else "place_early",
    )(*operands)


def gram_dot(a, b):
    return lax.dot_general(a, b, (((1,), (1,)), ((), ())), preferred_element_type=F32)


def four_planes(field, away, keep, smoothed, total_cells):
    across = [(1, 2), (2, 1)]
    inward = [(0, 1), (3, 2)]
    far_in = lax.ppermute(away, "dp", across)
    near_away = lax.ppermute(away, "dp", inward)
    near_keep = lax.ppermute(keep, "dp", inward)
    near_away, smoothed = lax.optimization_barrier((near_away, smoothed))
    far_out = lax.ppermute(near_away, "dp", across)
    scale = 1.0 / total_cells
    begun = gram_dot(near_away, away)
    early = [gram_dot(keep, far_in).astype(BF16), gram_dot(field, field).astype(BF16)]
    early = place(early, scale, False)
    near_keep, far_out, far_in, begun, early, smoothed = lax.optimization_barrier(
        (near_keep, far_out, far_in, begun, early, smoothed)
    )
    gram = place((near_keep, far_in, far_out, keep, begun, early), scale, True)
    return smoothed, gram


def ring(field, total_cells):
    rows = field.shape[0]
    count = lax.axis_size("dp")
    pos = lax.axis_index("dp")
    pairs = [(s, (s + 1) % count) for s in range(count)]
    block = jnp.zeros((rows, rows * count), F32)

    def add(block, panel, source):
        return lax.dynamic_update_slice(block, gram_dot(field, panel), (jnp.int32(0), source * rows))

    block = add(block, field, pos)

    def turn(i, carry):
        block, panel = carry
        panel = lax.ppermute(panel, "dp", pairs)
        return add(block, panel, (pos - i) % count), panel

    block, _ = lax.fori_loop(1, count, turn, (block, field))
    cols = block.shape[1] // lax.axis_size("tile")
    own = lax.psum_scatter(block.astype(BF16), "tile", scatter_dimension=1, tiled=True)
    return own.astype(F32) / total_cells


def shards(sensitivity, diffusivity):
    rows, layers, width, ny = sensitivity.shape
    total_cells = layers * width * ny * lax.axis_size("tile")
    coeff = coefficients(diffusivity)
    flat = sensitivity.reshape(rows, layers * width * ny)
    planes = lax.axis_size("dp") == 4 and lax.axis_size("tile") == 8 and rows == 512
    middle, *halves = two_steps(flat, *first_halo(sensitivity), coeff, width, planes)
    (smoothed,) = two_steps(middle, *flat_halo(middle, width), coeff, width, False)
    if planes:
        smoothed, gram = four_planes(
            middle, *halves, smoothed.reshape(sensitivity.shape), total_cells
        )
    else:
        gram = ring(middle, total_cells)
    return smoothed.reshape(sensitivity.shape), gram


def solution(mesh):
    in_specs = (P("dp", None, "tile", None), P(None, "tile", None))
    out_specs = (P("dp", None, "tile", None), P("dp", "tile"))
    return jax.shard_map(shards, mesh=mesh, in_specs=in_specs, out_specs=out_specs, check_vma=False)
```

```python
import jax
import jax.numpy as jnp
from jax import lax
from jax.experimental import pallas as pl
from jax.experimental.pallas import tpu as pltpu
from jax.sharding import PartitionSpec as P

STEPS = 4
HALF = 2
MESH = pl.DeviceIdType.MESH
F32 = jnp.float32
BF16 = jnp.bfloat16


def neighbours(block, dim, width, axis="tile"):
    count = lax.axis_size(axis)
    forward = [(i, i + 1) for i in range(count - 1)]
    backward = [(t, s) for s, t in forward]
    low = lax.ppermute(
        lax.slice_in_dim(block, block.shape[dim] - width, None, axis=dim), axis, forward
    )
    high = lax.ppermute(lax.slice_in_dim(block, 0, width, axis=dim), axis, backward)
    return low, high


def extended(block, dim, width):
    low, high = neighbours(block, dim, width)
    return jnp.concatenate([low, block, high], axis=dim)


def coefficients(diffusivity):
    layers, width, ny = diffusivity.shape
    d = extended(diffusivity, 1, HALF)
    tile, tiles = lax.axis_index("tile"), lax.axis_size("tile")
    c = d[:, 1:-1]
    xm = 0.5 * (c + d[:, :-2])
    xp = 0.5 * (c + d[:, 2:])
    cp = jnp.pad(c, ((1, 1), (0, 0), (0, 0)))
    lm = 0.5 * (c + cp[:-2])
    lp = 0.5 * (c + cp[2:])
    cy = jnp.pad(c, ((0, 0), (0, 0), (1, 1)))
    ym = 0.5 * (c + cy[:, :, :-2])
    yp = 0.5 * (c + cy[:, :, 2:])
    a0 = 1.0 - (xm + xp + lm + lp + ym + yp)
    lay = jnp.arange(layers)[:, None, None]
    col = jnp.arange(ny)[None, None, :]
    other = jnp.where(lay == 0, lp, lm)
    ym = jnp.where(col == 0, 0.0, ym)
    yp = jnp.where(col == ny - 1, 0.0, yp)
    x = jnp.arange(width + 2)[None, :, None]
    inside = ((x > 0) | (tile > 0)) & ((x < width + 1) | (tile < tiles - 1))
    stack = jnp.where(inside[None], jnp.stack([a0, xm, xp, other, ym, yp]), 0.0)
    return stack.reshape(6, layers * (width + 2), ny)


def smooth_kernel(width, split, main_ref, low_ref, high_ref, coeff_ref, out_ref, *halves):
    lanes = 128
    half = width * lanes

    def load(layer, x):
        if x < HALF:
            at = (layer * HALF + x) * lanes
            return low_ref[:, at : at + lanes].astype(F32)
        if x >= width + HALF:
            at = (layer * HALF + x - width - HALF) * lanes
            return high_ref[:, at : at + lanes].astype(F32)
        at = (layer * width + x - HALF) * lanes
        return main_ref[:, at : at + lanes].astype(F32)

    def step(read, layer, x, cx):
        at = layer * (width + 2) + cx
        w = [coeff_ref[i, at : at + 1, :] for i in range(6)]
        f = read(layer, x)
        total = w[0] * f + w[1] * read(layer, x - 1) + w[2] * read(layer, x + 1)
        total = total + w[3] * read(1 - layer, x)
        total = total + w[4] * pltpu.roll(f, 1, 1)
        return total + w[5] * pltpu.roll(f, lanes - 1, 1)

    first = {}

    def read_first(layer, x):
        if (layer, x) not in first:
            first[layer, x] = step(load, layer, x, x - 1)
        return first[layer, x]

    for x in range(HALF, width + HALF):
        for layer in range(2):
            value = step(read_first, layer, x, x - 1)
            at = (layer * width + x - HALF) * lanes
            out_ref[:, at : at + lanes] = value.astype(BF16)
    if split:
        away_ref, keep_ref = halves
        left = 2 * lax.axis_index("dp") < lax.axis_size("dp")

        @pl.when(left)
        def _():
            away_ref[...] = out_ref[:, :half]
            keep_ref[...] = out_ref[:, half:]

        @pl.when(jnp.logical_not(left))
        def _():
            away_ref[...] = out_ref[:, half:]
            keep_ref[...] = out_ref[:, :half]


def two_steps(main, low, high, coeff, width, split):
    rows, cells = main.shape
    block = 32
    outs = [cells] + ([cells // 2] * 2 if split else [])
    return pl.pallas_call(
        lambda *refs: smooth_kernel(width, split, *refs),
        out_shape=[jax.ShapeDtypeStruct((rows, n), BF16) for n in outs],
        grid=(rows // block,),
        in_specs=[
            pl.BlockSpec((block, cells), lambda i: (i, 0)),
            pl.BlockSpec((block, low.shape[1]), lambda i: (i, 0)),
            pl.BlockSpec((block, high.shape[1]), lambda i: (i, 0)),
            pl.BlockSpec(coeff.shape, lambda i: (0, 0, 0)),
        ],
        out_specs=[pl.BlockSpec((block, n), lambda i: (i, 0)) for n in outs],
        cost_estimate=pl.CostEstimate(
            flops=rows * cells * 24, bytes_accessed=rows * cells * 8, transcendentals=0
        ),
        name="two_steps",
    )(main, low, high, coeff)


def exchange(tops, bottoms):
    count = lax.axis_size("tile")
    forward = [(i, i + 1) for i in range(count - 1)]
    low = lax.ppermute(tops, "tile", forward)
    high = lax.ppermute(bottoms, "tile", [(t, s) for s, t in forward])
    return low, high


def flat_halo(flat, width):
    n = width * 128
    w = HALF * 128
    tops = jnp.concatenate([flat[:, n - w : n], flat[:, 2 * n - w :]], axis=1)
    bottoms = jnp.concatenate([flat[:, :w], flat[:, n : n + w]], axis=1)
    return exchange(tops, bottoms)


def first_halo(block):
    rows, width = block.shape[0], block.shape[2]
    return exchange(
        block[:, :, width - HALF :].reshape(rows, -1), block[:, :, :HALF].reshape(rows, -1)
    )


def place_kernel(scale, late, *refs):
    order = (1, 3, 0, 2, 4) if late else (5,)
    slot_of = {b: n for n, b in enumerate(order)}
    if late:
        near_ref, far_in_ref, far_out_ref, keep_ref, begun_ref, ready_ref, early_ref = refs[:7]
        refs = refs[7:]
    else:
        ready_ref, refs = refs[0], refs[1:]
    (out_ref, outgoing, own, partner, half_out, quarter, direct_out, turned_out, direct, turned,
     s1_send, s1_recv, s2_send, s2_recv, d_send, t_send, d_recv, t_recv) = refs

    def product(b, cols):
        if b in (1, 5):
            return ready_ref[:, cols].astype(F32)
        rows_ref = keep_ref if b == 2 else near_ref
        cols_ref = {0: keep_ref, 2: far_out_ref, 3: far_in_ref, 4: far_out_ref}[b]
        value = gram_dot(rows_ref[...], cols_ref[cols, :])
        return value + begun_ref[:, cols] if b == 0 else value
    p = lax.axis_index("dp")
    t = lax.axis_index("tile")
    tiles = 8
    u, v = t // 2, t % 2
    inner = (p == 1) | (p == 2)
    outer_of = jnp.where(p < 2, 0, 3)
    inner_of = jnp.where(p < 2, 1, 2)
    far_in = 3 - inner_of
    far_out = 3 - outer_of

    barrier = pltpu.get_barrier_semaphore()

    def greet(n, _):
        @pl.when(n != p * tiles + t)
        def _():
            pl.semaphore_signal(barrier, inc=1, device_id=(n // tiles, n % tiles), device_id_type=MESH)
        return 0

    lax.fori_loop(0, 32, greet, 0)
    pl.semaphore_wait(barrier, 31)

    def when_active(b, run):
        if b == 5:
            run()
        else:
            pl.when(inner)(run)

    own_cols = pl.ds(pl.multiple_of(v * 256, 256), 256)
    other_cols = pl.ds(pl.multiple_of((1 - v) * 256, 256), 256)
    own_rows = pl.ds(pl.multiple_of(u * 128, 128), 128)

    def stage1(b):
        n = slot_of[b]
        return pltpu.make_async_remote_copy(
            src_ref=outgoing.at[n], dst_ref=partner.at[n], send_sem=s1_send.at[n],
            recv_sem=s1_recv.at[n], device_id=(p, 2 * u + 1 - v), device_id_type=MESH)

    def stage2(b, k):
        n = slot_of[b]
        to = (u + k) % 4
        return pltpu.make_async_remote_copy(
            src_ref=half_out.at[n, pl.ds(pl.multiple_of(to * 128, 128), 128), :],
            dst_ref=quarter.at[n, k - 1], send_sem=s2_send.at[n, k - 1],
            recv_sem=s2_recv.at[n, k - 1], device_id=(p, 2 * to + v), device_id_type=MESH)

    rows_of = [outer_of, inner_of, inner_of, outer_of, outer_of, p]
    cols_of = [inner_of, far_in, far_out, far_in, far_out, p]

    def send_direct(b, action):
        dp, dt = rows_of[b], 2 * cols_of[b] + v
        active = inner if b < 5 else (p >= 0)
        mine = (dp == p) & (dt == t)
        where = direct.at[pl.ds(pl.multiple_of(u * 128, 128), 128), :]
        copy = pltpu.make_async_remote_copy(
            src_ref=direct_out.at[slot_of[b]], dst_ref=where, send_sem=d_send.at[slot_of[b]],
            recv_sem=d_recv.at[u], device_id=(dp, dt), device_id_type=MESH)

        @pl.when(active & jnp.logical_not(mine))
        def _():
            copy.start() if action == 0 else copy.wait_send()

        if action == 0:
            @pl.when(active & mine)
            def _():
                where[...] = direct_out[slot_of[b]]

    def send_turned(b, action):
        dp, dt = cols_of[b], 2 * rows_of[b] + u // 2
        mine = (dp == p) & (dt == t)
        col = u % 2
        slot = v * 2 + col
        copy = pltpu.make_async_remote_copy(
            src_ref=turned_out.at[slot_of[b]], dst_ref=turned.at[slot], send_sem=t_send.at[slot_of[b]],
            recv_sem=t_recv.at[slot], device_id=(dp, dt), device_id_type=MESH)

        @pl.when(inner & jnp.logical_not(mine))
        def _():
            copy.start() if action == 0 else copy.wait_send()

        if action == 0:
            @pl.when(inner & mine)
            def _():
                turned[slot] = turned_out[slot_of[b]]

    for b in order:
        def begin(b=b):
            outgoing[slot_of[b]] = product(b, other_cols).astype(BF16)
            stage1(b).start()
        when_active(b, begin)
    for b in order:
        def add_partner(b=b):
            n = slot_of[b]
            own[n] = product(b, own_cols)
            stage1(b).wait_recv()
            half_out[n] = (own[n] + partner[n].astype(F32)).astype(BF16)
            for k in range(1, 4):
                stage2(b, k).start()
        when_active(b, add_partner)
    for b in order:
        def finish(b=b):
            n = slot_of[b]
            value = own[n, own_rows, :] + partner[n, own_rows, :].astype(F32)
            for k in range(1, 4):
                stage2(b, k).wait_recv()
                value = value + quarter[n, k - 1].astype(F32)
            value = value * scale
            direct_out[n] = value.astype(BF16)
            if b < 5:
                turned_out[n] = value.T.astype(BF16)
        when_active(b, finish)
        send_direct(b, 0)
        if b < 5:
            send_turned(b, 0)

    g = t // 2
    same_side = (p < 2) == (g < 2)
    cross = jnp.logical_not(same_side)
    has_direct = cross | (p == g) | jnp.logical_not(inner)
    direct_from = jnp.where(p == g, p, inner_of)
    has_turned = cross | ((p != g) & inner)
    turned_from = jnp.where(cross, far_in, inner_of)
    early_cell = p == g
    mine_now = jnp.logical_not(early_cell) if late else early_cell
    has_direct = has_direct & mine_now
    has_turned = has_turned & mine_now
    if late:
        @pl.when(early_cell)
        def _():
            out_ref[...] = early_ref[...]
    else:
        @pl.when(jnp.logical_not(early_cell))
        def _():
            out_ref[...] = jnp.zeros_like(out_ref)

    @pl.when(has_direct)
    def _():
        for uu in range(4):
            @pl.when(jnp.logical_not((direct_from == p) & (2 * uu + v == t)))
            def _():
                pltpu.make_async_remote_copy(
                    src_ref=direct_out.at[0], dst_ref=direct.at[pl.ds(uu * 128, 128), :],
                    send_sem=d_send.at[0], recv_sem=d_recv.at[uu], device_id=(p, t),
                    device_id_type=MESH).wait_recv()
        out_ref[...] = direct[...].astype(F32)

    @pl.when(has_turned)
    def _():
        for vv in range(2):
            for cc in range(2):
                @pl.when(jnp.logical_not((turned_from == p) & (2 * (2 * v + cc) + vv == t)))
                def _():
                    pltpu.make_async_remote_copy(
                        src_ref=turned_out.at[0], dst_ref=turned.at[vv * 2 + cc],
                        send_sem=t_send.at[0], recv_sem=t_recv.at[vv * 2 + cc], device_id=(p, t),
                        device_id_type=MESH).wait_recv()

    for vv in range(2):
        for cc in range(2):
            rr, ll = slice(vv * 256, vv * 256 + 256), slice(cc * 128, cc * 128 + 128)

            @pl.when(has_turned & has_direct)
            def _():
                out_ref[rr, ll] += turned[vv * 2 + cc].astype(F32)

            @pl.when(has_turned & jnp.logical_not(has_direct))
            def _():
                out_ref[rr, ll] = turned[vv * 2 + cc].astype(F32)

    for b in order:
        def sent(b=b):
            stage1(b).wait_send()
            for k in range(1, 4):
                stage2(b, k).wait_send()
        when_active(b, sent)
        send_direct(b, 1)
        if b < 5:
            send_turned(b, 1)


def place(operands, scale, late):
    n = 5 if late else 1
    return pl.pallas_call(
        lambda *refs: place_kernel(scale, late, *refs),
        out_shape=jax.ShapeDtypeStruct((512, 256), F32),
        in_specs=[pl.BlockSpec(memory_space=pltpu.VMEM)] * len(operands),
        out_specs=pl.BlockSpec(memory_space=pltpu.VMEM),
        scratch_shapes=[
            pltpu.VMEM((n, 512, 256), BF16),
            pltpu.VMEM((n, 512, 256), F32),
            pltpu.VMEM((n, 512, 256), BF16),
            pltpu.VMEM((n, 512, 256), BF16),
            pltpu.VMEM((n, 3, 128, 256), BF16),
            pltpu.VMEM((n, 128, 256), BF16),
            pltpu.VMEM((n, 256, 128), BF16),
            pltpu.VMEM((512, 256), BF16),
            pltpu.VMEM((4, 256, 128), BF16),
            pltpu.SemaphoreType.DMA((n,)),
            pltpu.SemaphoreType.DMA((n,)),
            pltpu.SemaphoreType.DMA((n, 3)),
            pltpu.SemaphoreType.DMA((n, 3)),
            pltpu.SemaphoreType.DMA((n,)),
            pltpu.SemaphoreType.DMA((n,)),
            pltpu.SemaphoreType.DMA((4,)),
            pltpu.SemaphoreType.DMA((4,)),
        ],
        compiler_params=pltpu.CompilerParams(
            collective_id=int(late), has_side_effects=True, vmem_limit_bytes=40 * 1024 * 1024
        ),
        cost_estimate=pl.CostEstimate(flops=0, bytes_accessed=50_000_000, transcendentals=0),
        name="place_late" if late else "place_early",
    )(*operands)


def gram_dot(a, b):
    return lax.dot_general(a, b, (((1,), (1,)), ((), ())), preferred_element_type=F32)


def four_planes(field, away, keep, smoothed, total_cells):
    across = [(1, 2), (2, 1)]
    inward = [(0, 1), (3, 2)]
    far_in = lax.ppermute(away, "dp", across)
    near_away = lax.ppermute(away, "dp", inward)
    near_keep = lax.ppermute(keep, "dp", inward)
    near_away, smoothed = lax.optimization_barrier((near_away, smoothed))
    far_out = lax.ppermute(near_away, "dp", across)
    scale = 1.0 / total_cells
    begun = gram_dot(near_away, away)
    ready = gram_dot(keep, far_in).astype(BF16)
    early = place([gram_dot(field, field).astype(BF16)], scale, False)
    near_keep, far_out, far_in, begun, ready, early, smoothed = lax.optimization_barrier(
        (near_keep, far_out, far_in, begun, ready, early, smoothed)
    )
    gram = place((near_keep, far_in, far_out, keep, begun, ready, early), scale, True)
    return smoothed, gram


def ring(field, total_cells):
    rows = field.shape[0]
    count = lax.axis_size("dp")
    pos = lax.axis_index("dp")
    pairs = [(s, (s + 1) % count) for s in range(count)]
    block = jnp.zeros((rows, rows * count), F32)

    def add(block, panel, source):
        return lax.dynamic_update_slice(block, gram_dot(field, panel), (jnp.int32(0), source * rows))

    block = add(block, field, pos)

    def turn(i, carry):
        block, panel = carry
        panel = lax.ppermute(panel, "dp", pairs)
        return add(block, panel, (pos - i) % count), panel

    block, _ = lax.fori_loop(1, count, turn, (block, field))
    cols = block.shape[1] // lax.axis_size("tile")
    own = lax.psum_scatter(block.astype(BF16), "tile", scatter_dimension=1, tiled=True)
    return own.astype(F32) / total_cells


def shards(sensitivity, diffusivity):
    rows, layers, width, ny = sensitivity.shape
    total_cells = layers * width * ny * lax.axis_size("tile")
    coeff = coefficients(diffusivity)
    flat = sensitivity.reshape(rows, layers * width * ny)
    planes = lax.axis_size("dp") == 4 and lax.axis_size("tile") == 8 and rows == 512
    middle, *halves = two_steps(flat, *first_halo(sensitivity), coeff, width, planes)
    (smoothed,) = two_steps(middle, *flat_halo(middle, width), coeff, width, False)
    if planes:
        smoothed, gram = four_planes(
            middle, *halves, smoothed.reshape(sensitivity.shape), total_cells
        )
    else:
        gram = ring(middle, total_cells)
    return smoothed.reshape(sensitivity.shape), gram


def solution(mesh):
    in_specs = (P("dp", None, "tile", None), P(None, "tile", None))
    out_specs = (P("dp", None, "tile", None), P("dp", "tile"))
    return jax.shard_map(shards, mesh=mesh, in_specs=in_specs, out_specs=out_specs, check_vma=False)
```
